32 devices in a mesh: segment: 4 (over y, x), col: 8 (over z, core).
Axes of the slice: x: 2, y: 2, z: 4, core: 2. Of those that a mesh axis runs over, the one named last changes fastest.
Arguments:
- left_env: bfloat16 [384, 8192], P(None, 'col'), may hold values from -6 to 6
- bit_strings: int32 [384, 4], P(None, 'segment'), may hold values from 0 to 1
- site_tensors: bfloat16 [4, 2, 8192, 8192], P('segment', None, None, 'col'), may hold values from -0.0625 to 0.0625
Outputs:
- section_env: bfloat16 [4, 384, 8192], P('segment', None, 'col')
- section_log: float32 [4, 384], P('segment')
The draws below stay inside these ranges and needn't reach their ends.
All inputs are finite; a program needn't handle non-finite values. Where the reference program divides by a largest or mean magnitude, that divisor is 1e-20 or more.
Results may differ from the reference program's by a relative error of at most 0.0065.
Values may be sent and summed in bfloat16 or wider, within the bound.
A program may use at most 128 MiB of HBM per device.

```python
import jax
import jax.numpy as jnp
from jax import lax

CHI = 8192
PHYS = 2
ROWS = 384
SITES_SEGMENT = 1
SECTIONS = 4
SITES = 4


def touch_ends(array, key, smallest, largest):
    spot = [jax.random.randint(jax.random.fold_in(key, axis), (), 0, length) for axis, length in enumerate(array.shape)]
    main_axis = array.shape.index(max(array.shape))
    neighbour = spot[:main_axis] + [(spot[main_axis] + 1) % array.shape[main_axis]] + spot[main_axis + 1:]
    return array.at[tuple(spot)].set(smallest).at[tuple(neighbour)].set(largest)


def steps_of(stream_key, dims, cuts, low, largest):
    gain = 1.0
    for dim, blocks in cuts:
        steps = jax.random.uniform(jax.random.fold_in(jax.random.fold_in(stream_key, 6), dim), (blocks,), jnp.float32, low / len(cuts), largest / len(cuts))
        gain = gain * jnp.repeat(jnp.exp(steps), dims[dim] // blocks).reshape((-1,) + (1,) * (len(dims) - 1 - dim))
    return gain


def bell_draw(key, dims, scale, limit, shards=(), held_as=jnp.bfloat16):
    result = jax.random.normal(key, dims, jnp.float32) * scale
    if len(shards) > 0:
        result = steps_of(key, dims, shards, -0.22, 0.18) * result
    return jnp.clip(result, min=-limit, max=limit).astype(held_as)


def setup_inputs(seed: int = 0) -> dict:
    streams_of = jax.random.split(jax.random.key(seed), 4)
    left_env = bell_draw(streams_of[0], (ROWS, CHI), 1.0, 6.0, ((1, 8),))
    bit_strings = touch_ends(jax.random.randint(streams_of[1], (ROWS, SITES), 0, 2), jax.random.fold_in(streams_of[1], 1), 0, 1).astype(jnp.int32)
    site_tensors = bell_draw(streams_of[2], (SITES, PHYS, CHI, CHI), CHI ** -0.5, 0.0625, ((0, 4), (3, 8)))
    return dict(left_env=left_env, bit_strings=bit_strings, site_tensors=site_tensors)


def reference(left_env, bit_strings, site_tensors):
    vector = left_env
    env_list = []
    log_list = []
    for section in range(SECTIONS):
        log_total = jnp.zeros((ROWS,), jnp.float32)
        for inner in range(SITES_SEGMENT):
            site_index = section * SITES_SEGMENT + inner
            operand = vector.astype(jnp.float32)
            product_zero = jnp.dot(operand, site_tensors[site_index, 0].astype(jnp.float32), precision=lax.Precision.HIGHEST)
            product_one = jnp.dot(operand, site_tensors[site_index, 1].astype(jnp.float32), precision=lax.Precision.HIGHEST)
            chosen = jnp.where(bit_strings[:, site_index:site_index + 1] == 1, product_one, product_zero)
            maximum = jnp.max(jnp.abs(chosen), axis=1) + jnp.float32(1e-6)
            vector = (chosen / maximum[:, None]).astype(jnp.bfloat16)
            log_total = log_total + jnp.log(maximum)
        env_list.append(vector)
        log_list.append(log_total)
    return jnp.stack(env_list), jnp.stack(log_list)
```

```python
import functools

import jax
import jax.numpy as jnp
from jax import lax
from jax.experimental import pallas as pl
from jax.experimental.pallas import tpu as pltpu
from jax.sharding import PartitionSpec as P

GRANULES = 8
EPSILON = 1e-06
MESH = pl.DeviceIdType.MESH


def granules_of(rows):
    for count in range(GRANULES, 0, -1):
        if rows % count == 0 and (rows // count) % 16 == 0:
            return count
    return 1


def chip_at(step, z, n):
    below, above = z, n - 1 - z
    both = jnp.minimum(below, above)
    paired = (step + 1) // 2
    near = jnp.where(step % 2 == 1, z - paired, z + paired)
    far = jnp.where(below < above, z + (step - both), z - (step - both))
    return jnp.where(step <= 2 * both, near, far)


def kernel(
    stages, peers, granules,
    env_in, bits_in, tensor_in, env_out, log_out,
    weights, pieces, product, outgoing, peak, peak_sent, peak_all, scale_in, scale_sent,
    load_sem, weight_sem, arrive_sem, up_sem, down_sem, cross_sem, next_sem,
    peak_send_sem, peak_recv_sem, scale_send_sem, scale_recv_sem,
):
    rows, width = outgoing.shape
    block = rows // granules
    n = peers // 2
    stage = lax.axis_index("segment")
    me = lax.axis_index("col")
    z = me // 2
    core = me % 2

    def there(segment, col):
        return {"segment": segment, "col": col}

    load = pltpu.make_async_copy(env_in, pieces.at[me], load_sem)

    @pl.when(stage == 0)
    def _():
        load.start()

    def owner_at(step):
        chip = chip_at(step // 2, z, n)
        return chip, chip * 2 + jnp.where(step % 2 == 0, core, 1 - core)

    def weight_copy(owner):
        return pltpu.make_async_copy(
            tensor_in.at[0, :, pl.ds(pl.multiple_of(owner * width, width), width), :],
            weights.at[owner],
            weight_sem.at[owner],
        )

    def start_weight(step, carry):
        weight_copy(owner_at(step)[1]).start()
        return carry

    lax.fori_loop(0, peers, start_weight, 0)

    barrier = pltpu.get_barrier_semaphore()

    def greet(by, carry):
        pl.semaphore_signal(
            barrier, inc=1, device_id=there(stage, (me + by) % peers), device_id_type=MESH
        )
        return carry

    lax.fori_loop(1, peers, greet, 0)

    @pl.when(stage > 0)
    def _():
        pl.semaphore_signal(barrier, inc=1, device_id=there(stage - 1, me), device_id_type=MESH)

    @pl.when(stage < stages - 1)
    def _():
        pl.semaphore_signal(barrier, inc=1, device_id=there(stage + 1, me), device_id_type=MESH)

    neighbours = jnp.where(stage > 0, 1, 0) + jnp.where(stage < stages - 1, 1, 0)
    pl.semaphore_wait(barrier, peers - 1 + neighbours)

    @pl.when(stage == 0)
    def _():
        load.wait()

    def rows_of(granule):
        return pl.ds(pl.multiple_of(granule * block, block), block)

    def piece(granule, owner):
        return pieces.at[owner, rows_of(granule), :]

    def along(granule, owner, send, col):
        part = piece(granule, owner)
        return pltpu.make_async_remote_copy(
            src_ref=part,
            dst_ref=part,
            send_sem=send.at[granule, owner // 2],
            recv_sem=arrive_sem.at[granule, owner],
            device_id=there(stage, col),
            device_id_type=MESH,
        )

    def up(granule, owner):
        return along(granule, owner, up_sem, me + 2)

    def down(granule, owner):
        return along(granule, owner, down_sem, me - 2)

    def cross(granule, owner):
        return along(granule, owner, cross_sem, 2 * z + 1 - core)

    def onward(granule):
        return pltpu.make_async_remote_copy(
            src_ref=outgoing.at[rows_of(granule), :],
            dst_ref=piece(granule, me),
            send_sem=next_sem.at[granule],
            recv_sem=arrive_sem.at[granule, me],
            device_id=there(stage + 1, me),
            device_id_type=MESH,
        )

    def one_granule(granule, carry):
        bit = bits_in[rows_of(granule), :].astype(jnp.float32).astype(jnp.bfloat16)

        def one_piece(step, carry):
            chip, owner = owner_at(step)

            @pl.when((stage > 0) | (step > 0))
            def _():
                along(granule, owner, cross_sem, 2 * z + 1 - core).wait_recv()

            @pl.when(step % 2 == 0)
            def _():
                @pl.when((chip <= z) & (z < n - 1))
                def _():
                    up(granule, owner).start()

                @pl.when((chip >= z) & (z > 0))
                def _():
                    down(granule, owner).start()

                cross(granule, owner).start()

            @pl.when(granule == 0)
            def _():
                weight_copy(owner).wait()

            value = piece(granule, owner)[...]
            one = value * bit
            both = jnp.concatenate([value - one, one], axis=1)
            part = jnp.dot(
                both,
                weights[owner].reshape(2 * width, width),
                preferred_element_type=jnp.float32,
            )

            @pl.when(step == 0)
            def _():
                product[rows_of(granule), :] = part

            @pl.when(step > 0)
            def _():
                product[rows_of(granule), :] += part

            return carry

        lax.fori_loop(0, peers, one_piece, 0)
        done = product[rows_of(granule), :]
        outgoing[rows_of(granule), :] = done.astype(jnp.bfloat16)

        @pl.when(stage < stages - 1)
        def _():
            onward(granule).start()

        largest = jnp.max(jnp.abs(done), axis=1, keepdims=True)
        peak[rows_of(granule), :] = jnp.broadcast_to(largest, (block, peak.shape[1]))
        return carry

    lax.fori_loop(0, granules, one_granule, 0)

    mine = jnp.transpose(peak[...])[:8]
    peak_sent[...] = mine

    def peak_copy(by):
        return pltpu.make_async_remote_copy(
            src_ref=peak_sent,
            dst_ref=peak_all.at[by],
            send_sem=peak_send_sem.at[by],
            recv_sem=peak_recv_sem.at[by],
            device_id=there(stage, (me + by) % peers),
            device_id_type=MESH,
        )

    def start_peak(by, carry):
        peak_copy(by).start()
        return carry

    lax.fori_loop(1, peers, start_peak, 0)

    scale_copy = pltpu.make_async_remote_copy(
        src_ref=scale_sent,
        dst_ref=scale_in,
        send_sem=scale_send_sem,
        recv_sem=scale_recv_sem,
        device_id=there(stage + 1, me),
        device_id_type=MESH,
    )

    @pl.when(stage == 0)
    def _():
        scale_in[...] = jnp.ones_like(scale_in)

    @pl.when(stage > 0)
    def _():
        scale_copy.wait_recv()

    def take_peak(by, largest):
        peak_copy(by).wait_recv()
        return jnp.maximum(largest, peak_all[by])

    largest = lax.fori_loop(1, peers, take_peak, mine)
    before = scale_in[...]
    scale = largest + EPSILON * before
    scale_sent[...] = scale

    @pl.when(stage < stages - 1)
    def _():
        scale_copy.start()

    log_out[...] = jnp.log(largest / before + EPSILON)[:1]
    by_row = jnp.transpose(jnp.broadcast_to(scale[:1], (128, rows)))[:, :1]
    env_out[0] = (product[...] / by_row).astype(jnp.bfloat16)

    def drain(granule, carry):
        def drain_chip(chip, carry):
            owner = chip * 2 + core

            @pl.when((chip <= z) & (z < n - 1))
            def _():
                up(granule, owner).wait_send()

            @pl.when((chip >= z) & (z > 0))
            def _():
                down(granule, owner).wait_send()

            cross(granule, owner).wait_send()
            return carry

        lax.fori_loop(0, n, drain_chip, 0)

        @pl.when(stage < stages - 1)
        def _():
            onward(granule).wait_send()

        return carry

    lax.fori_loop(0, granules, drain, 0)

    def drain_peak(by, carry):
        peak_copy(by).wait_send()
        return carry

    lax.fori_loop(1, peers, drain_peak, 0)

    @pl.when(stage < stages - 1)
    def _():
        scale_copy.wait_send()


def solution(mesh):
    stages, peers = mesh.shape["segment"], mesh.shape["col"]
    n = peers // 2

    def local(left_env, bit_strings, site_tensors):
        rows, width = left_env.shape
        granules = granules_of(rows)
        vmem = pl.BlockSpec(memory_space=pltpu.VMEM)
        anywhere = pl.BlockSpec(memory_space=pl.ANY)
        dma = pltpu.SemaphoreType.DMA
        return pl.pallas_call(
            functools.partial(kernel, stages, peers, granules),
            out_shape=(
                jax.ShapeDtypeStruct((1, rows, width), jnp.bfloat16),
                jax.ShapeDtypeStruct((1, rows), jnp.float32),
            ),
            in_specs=[anywhere, vmem, anywhere],
            out_specs=(vmem, vmem),
            scratch_shapes=[
                pltpu.VMEM((peers, 2, width, width), jnp.bfloat16),
                pltpu.VMEM((peers, rows, width), jnp.bfloat16),
                pltpu.VMEM((rows, width), jnp.float32),
                pltpu.VMEM((rows, width), jnp.bfloat16),
                pltpu.VMEM((rows, 128), jnp.float32),
                pltpu.VMEM((8, rows), jnp.float32),
                pltpu.VMEM((peers, 8, rows), jnp.float32),
                pltpu.VMEM((8, rows), jnp.float32),
                pltpu.VMEM((8, rows), jnp.float32),
                dma,
                dma((peers,)),
                dma((granules, peers)),
                dma((granules, n)),
                dma((granules, n)),
                dma((granules, n)),
                dma((granules,)),
                dma((peers,)),
                dma((peers,)),
                dma,
                dma,
            ],
            compiler_params=pltpu.CompilerParams(
                collective_id=0, has_side_effects=True, vmem_limit_bytes=60 * 1024 * 1024
            ),
        )(left_env, bit_strings, site_tensors)

    return jax.shard_map(
        local,
        mesh=mesh,
        in_specs=(P(None, "col"), P(None, "segment"), P("segment", None, None, "col")),
        out_specs=(P("segment", None, "col"), P("segment", None)),
        check_vma=False,
    )
```

```python
import functools

import jax
import jax.numpy as jnp
from jax import lax
from jax.experimental import pallas as pl
from jax.experimental.pallas import tpu as pltpu
from jax.sharding import PartitionSpec as P

GRANULES = 12
DIRECT = True
EPSILON = 1e-06
MESH = pl.DeviceIdType.MESH


def granules_of(rows):
    for count in range(GRANULES, 0, -1):
        if rows % count == 0 and (rows // count) % 16 == 0:
            return count
    return 1


def chip_at(step, z, n):
    below, above = z, n - 1 - z
    both = jnp.minimum(below, above)
    paired = (step + 1) // 2
    near = jnp.where(step % 2 == 1, z - paired, z + paired)
    far = jnp.where(below < above, z + (step - both), z - (step - both))
    return jnp.where(step <= 2 * both, near, far)


def kernel(
    stages, peers, granules,
    env_in, bits_in, tensor_in, env_out, log_out,
    weights, pieces, product, outgoing, peak, peak_sent, peak_all, scale_in, scale_sent,
    load_sem, weight_sem, arrive_sem, line_sem, cross_sem, next_sem,
    peak_send_sem, peak_recv_sem, scale_send_sem, scale_recv_sem,
):
    rows, width = outgoing.shape
    block = rows // granules
    n = peers // 2
    stage = lax.axis_index("segment")
    me = lax.axis_index("col")
    z = me // 2
    core = me % 2

    def there(segment, col):
        return {"segment": segment, "col": col}

    load = pltpu.make_async_copy(env_in, pieces.at[me], load_sem)

    @pl.when(stage == 0)
    def _():
        load.start()

    def owner_at(step):
        chip = chip_at(step % n, z, n)
        return chip, chip * 2 + jnp.where(step < n, core, 1 - core)

    def weight_copy(owner):
        return pltpu.make_async_copy(
            tensor_in.at[0, :, pl.ds(pl.multiple_of(owner * width, width), width), :],
            weights.at[owner],
            weight_sem.at[owner],
        )

    def start_weight(step, carry):
        weight_copy(owner_at(step)[1]).start()
        return carry

    lax.fori_loop(0, peers, start_weight, 0)

    barrier = pltpu.get_barrier_semaphore()

    def greet(by, carry):
        pl.semaphore_signal(
            barrier, inc=1, device_id=there(stage, (me + by) % peers), device_id_type=MESH
        )
        return carry

    lax.fori_loop(1, peers, greet, 0)

    count = jnp.int32(0)
    for by in (-2, -1, 0, 1, 2):
        inside = (z + by >= 0) & (z + by < n)
        for other in (-1, 1):
            meets = inside & (stage + other >= 0) & (stage + other < stages)

            @pl.when(meets)
            def _():
                pl.semaphore_signal(
                    barrier,
                    inc=1,
                    device_id=there(stage + other, me + 2 * by),
                    device_id_type=MESH,
                )

            count = count + jnp.where(meets, 1, 0)
    pl.semaphore_wait(barrier, peers - 1 + count)

    @pl.when(stage == 0)
    def _():
        load.wait()

    def rows_of(granule):
        return pl.ds(pl.multiple_of(granule * block, block), block)

    def piece(granule, owner):
        return pieces.at[owner, rows_of(granule), :]

    def send(source, granule, owner, sem, segment, col):
        return pltpu.make_async_remote_copy(
            src_ref=source,
            dst_ref=piece(granule, owner),
            send_sem=sem,
            recv_sem=arrive_sem.at[granule, owner],
            device_id=there(segment, col),
            device_id_type=MESH,
        )

    def cross(granule, owner):
        col = 2 * z + 1 - core
        return send(
            piece(granule, owner), granule, owner, cross_sem.at[granule, owner // 2], stage, col
        )

    def along(act, granule, chip):
        owner = chip * 2 + core
        source = piece(granule, owner)
        for slot, by in enumerate((1, -1, 2, -2)):
            ahead = chip <= z if by > 0 else chip >= z
            if DIRECT:
                ahead = ahead & ((chip != z) | (stage == 0))

            @pl.when(ahead & ((z - chip) % 2 == 0) & (z + by >= 0) & (z + by < n))
            def _():
                sem = line_sem.at[slot, granule, chip]
                act(send(source, granule, owner, sem, stage, me + 2 * by))

    def onward(act, granule):
        source = outgoing.at[rows_of(granule), :]
        for slot, by in enumerate((0, 1, -1, 2, -2) if DIRECT else (0,)):

            @pl.when((stage < stages - 1) & (z + by >= 0) & (z + by < n))
            def _():
                sem = next_sem.at[slot, granule]
                act(send(source, granule, me, sem, stage + 1, me + 2 * by))

    def start(copy):
        copy.start()

    def sent(copy):
        copy.wait_send()

    def open_granule(granule):
        @pl.when(stage == 0)
        def _():
            along(start, granule, z)
            cross(granule, me).start()

    open_granule(0)

    def one_granule(granule, carry):
        @pl.when(granule + 1 < granules)
        def _():
            open_granule(granule + 1)

        bit = bits_in[rows_of(granule), :].astype(jnp.float32).astype(jnp.bfloat16)

        def one_piece(step, carry):
            chip, owner = owner_at(step)

            @pl.when((stage > 0) | (step > 0))
            def _():
                cross(granule, owner).wait_recv()

                @pl.when(step < n)
                def _():
                    along(start, granule, chip)
                    cross(granule, owner).start()

            @pl.when(granule == 0)
            def _():
                weight_copy(owner).wait()

            value = piece(granule, owner)[...]
            one = value * bit
            both = jnp.concatenate([value - one, one], axis=1)
            part = jnp.dot(
                both,
                weights[owner].reshape(2 * width, width),
                preferred_element_type=jnp.float32,
            )

            @pl.when(step == 0)
            def _():
                product[rows_of(granule), :] = part

            @pl.when(step > 0)
            def _():
                product[rows_of(granule), :] += part

            return carry

        lax.fori_loop(0, peers, one_piece, 0)
        done = product[rows_of(granule), :]
        outgoing[rows_of(granule), :] = done.astype(jnp.bfloat16)

        onward(start, granule)

        largest = jnp.max(jnp.abs(done), axis=1, keepdims=True)
        peak[rows_of(granule), :] = jnp.broadcast_to(largest, (block, peak.shape[1]))
        return carry

    lax.fori_loop(0, granules, one_granule, 0)

    mine = jnp.transpose(peak[...])[:8]
    peak_sent[...] = mine

    def peak_copy(by):
        return pltpu.make_async_remote_copy(
            src_ref=peak_sent,
            dst_ref=peak_all.at[by],
            send_sem=peak_send_sem.at[by],
            recv_sem=peak_recv_sem.at[by],
            device_id=there(stage, (me + by) % peers),
            device_id_type=MESH,
        )

    def start_peak(by, carry):
        peak_copy(by).start()
        return carry

    lax.fori_loop(1, peers, start_peak, 0)

    scale_copy = pltpu.make_async_remote_copy(
        src_ref=scale_sent,
        dst_ref=scale_in,
        send_sem=scale_send_sem,
        recv_sem=scale_recv_sem,
        device_id=there(stage + 1, me),
        device_id_type=MESH,
    )

    @pl.when(stage == 0)
    def _():
        scale_in[...] = jnp.ones_like(scale_in)

    @pl.when(stage > 0)
    def _():
        scale_copy.wait_recv()

    def take_peak(by, largest):
        peak_copy(by).wait_recv()
        return jnp.maximum(largest, peak_all[by])

    largest = lax.fori_loop(1, peers, take_peak, mine)
    before = scale_in[...]
    scale = largest + EPSILON * before
    scale_sent[...] = scale

    @pl.when(stage < stages - 1)
    def _():
        scale_copy.start()

    log_out[...] = jnp.log(largest / before + EPSILON)[:1]
    by_row = jnp.transpose(jnp.broadcast_to(scale[:1], (128, rows)))[:, :1]
    env_out[0] = (product[...] / by_row).astype(jnp.bfloat16)

    def drain(granule, carry):
        def drain_chip(chip, carry):
            along(sent, granule, chip)
            cross(granule, chip * 2 + core).wait_send()
            return carry

        lax.fori_loop(0, n, drain_chip, 0)
        onward(sent, granule)
        return carry

    lax.fori_loop(0, granules, drain, 0)

    def drain_peak(by, carry):
        peak_copy(by).wait_send()
        return carry

    lax.fori_loop(1, peers, drain_peak, 0)

    @pl.when(stage < stages - 1)
    def _():
        scale_copy.wait_send()


def solution(mesh):
    stages, peers = mesh.shape["segment"], mesh.shape["col"]
    n = peers // 2

    def local(left_env, bit_strings, site_tensors):
        rows, width = left_env.shape
        granules = granules_of(rows)
        vmem = pl.BlockSpec(memory_space=pltpu.VMEM)
        anywhere = pl.BlockSpec(memory_space=pl.ANY)
        dma = pltpu.SemaphoreType.DMA
        return pl.pallas_call(
            functools.partial(kernel, stages, peers, granules),
            out_shape=(
                jax.ShapeDtypeStruct((1, rows, width), jnp.bfloat16),
                jax.ShapeDtypeStruct((1, rows), jnp.float32),
            ),
            in_specs=[anywhere, vmem, anywhere],
            out_specs=(vmem, vmem),
            scratch_shapes=[
                pltpu.VMEM((peers, 2, width, width), jnp.bfloat16),
                pltpu.VMEM((peers, rows, width), jnp.bfloat16),
                pltpu.VMEM((rows, width), jnp.float32),
                pltpu.VMEM((rows, width), jnp.bfloat16),
                pltpu.VMEM((rows, 128), jnp.float32),
                pltpu.VMEM((8, rows), jnp.float32),
                pltpu.VMEM((peers, 8, rows), jnp.float32),
                pltpu.VMEM((8, rows), jnp.float32),
                pltpu.VMEM((8, rows), jnp.float32),
                dma,
                dma((peers,)),
                dma((granules, peers)),
                dma((4, granules, n)),
                dma((granules, n)),
                dma((5, granules)),
                dma((peers,)),
                dma((peers,)),
                dma,
                dma,
            ],
            compiler_params=pltpu.CompilerParams(
                collective_id=0, has_side_effects=True, vmem_limit_bytes=60 * 1024 * 1024
            ),
        )(left_env, bit_strings, site_tensors)

    return jax.shard_map(
        local,
        mesh=mesh,
        in_specs=(P(None, "col"), P(None, "segment"), P("segment", None, None, "col")),
        out_specs=(P("segment", None, "col"), P("segment", None)),
        check_vma=False,
    )
```
